32 devices in a mesh: pts: 8 (over y, x, core), tau: 4 (over z).
Axes of the slice: x: 2, y: 2, z: 4, core: 2. Of those that a mesh axis runs over, the one named last changes fastest.
Arguments:
- occ_orbitals: bfloat16 [3072, 2048], P('pts'), may hold values from -1 to 1
- virt_orbitals: bfloat16 [3072, 4096], P('pts'), may hold values from -1 to 1
- potentials: bfloat16 [3072, 256], P('pts'), may hold values from -1 to 1
- occ_energy: float32 [2048], replicated, may hold values from -1 to -0.1
- virt_energy: float32 [4096], replicated, may hold values from 0.1 to 1
- times: float32 [4], P('tau'), may hold values from 0.25 to 4
- weights: float32 [4, 4], P(None, 'tau'), may hold values from -3 to 3
Outputs:
- screened: float32 [4, 256, 256], P('tau')
The draws below stay inside these ranges and needn't reach their ends.
All inputs are finite; a program needn't handle non-finite values.
Results may differ from the reference program's by a relative error of at most 0.0003.
Values may be sent and summed in bfloat16 or wider, within the bound.
No kernel may reach another device: no remote copies, remote signals or barrier semaphores. Data moves between devices by JAX's collectives and lax.ppermute only.
A program may use at most 128 MiB of HBM per device.

```python
import math
import jax
import jax.numpy as jnp
from jax import lax

NOCC = 2048
NVIRT = 4096
NPOT = 256
P_DEV = 384
NP = 3072
TIMES = 4
FREQS = 4


def rough_values(key, rows, columns):
    return jax.random.normal(key, (rows, columns), jnp.float32)


def common_rows(key, columns):
    shared_key, own_key = jax.random.split(key)
    shared_part = rough_values(shared_key, P_DEV, columns)
    shared_whole = jnp.tile(shared_part, (NP // P_DEV, 1))
    own_part = rough_values(own_key, NP, columns)
    return (shared_whole, own_part)


def orbital_panel(key, columns):
    spread_key, rows_key = jax.random.split(key)
    spread = jnp.exp(jax.random.uniform(spread_key, (columns,), jnp.float32, math.log(0.5), 0.0))
    shared_whole, own_part = common_rows(rows_key, columns)
    mixed = 0.7 * shared_whole + 0.7 * own_part
    panel_values = mixed * spread / jnp.sqrt(columns * 0.541)
    return jnp.clip(panel_values, -1.0, 1.0).astype(jnp.bfloat16)


def draw_occ_orbitals(key, part):
    return orbital_panel(jax.random.fold_in(key, 11), NOCC)


def draw_virt_orbitals(key, part):
    return orbital_panel(jax.random.fold_in(key, 23), NVIRT)


def draw_potentials(key, part):
    shared_whole, own_part = common_rows(jax.random.fold_in(key, 37), NPOT)
    mixed = (0.5 * shared_whole + 0.5 * own_part) / jnp.sqrt(1.0 * P_DEV)
    return jnp.clip(mixed, -1.0, 1.0).astype(jnp.bfloat16)


def block_scale(rng, extent, cuts, smallest, largest):
    factor_of = 1.0
    for axis_at, parts in cuts:
        heights = jax.random.uniform(jax.random.fold_in(jax.random.fold_in(rng, 6), axis_at), (parts,), jnp.float32, smallest / len(cuts), largest / len(cuts))
        factor_of = factor_of * jnp.repeat(jnp.exp(heights), extent[axis_at] // parts).reshape((-1,) + (1,) * (len(extent) - 1 - axis_at))
    return factor_of


def noise(key, extent, scale, bound, shards=(), held_as=jnp.bfloat16):
    entries = jax.random.normal(key, extent, jnp.float32) * scale
    if len(shards) > 0:
        entries = block_scale(key, extent, shards, -0.22, 0.18) * entries
    return jnp.clip(entries, min=-bound, max=bound).astype(held_as)


def setup_inputs(seed: int = 0) -> dict:
    key_of = jax.random.split(jax.random.key(seed), 8)
    occ_orbitals = draw_occ_orbitals(jax.random.fold_in(key_of[7], 71), 0)
    virt_orbitals = draw_virt_orbitals(jax.random.fold_in(key_of[7], 71), 0)
    potentials = draw_potentials(jax.random.fold_in(key_of[7], 71), 0)
    occ_energy = jnp.clip(jax.random.uniform(key_of[3], (NOCC,), jnp.float32, -1.0, -0.1), -1.0, -0.1)
    virt_energy = jnp.clip(jax.random.uniform(key_of[4], (NVIRT,), jnp.float32, 0.1, 1.0), 0.1, 1.0)
    times = jnp.clip(jnp.exp(math.log(4.0) - 2.7725887 * jax.random.uniform(key_of[5], (TIMES,), jnp.float32) ** block_scale(key_of[5], (TIMES,), ((0, 4),), -0.2, 0.2)), 0.25, 4.0)
    weights = noise(key_of[6], (FREQS, TIMES), TIMES ** -0.5, 3.0, ((1, 4),), jnp.float32)
    return {"occ_orbitals": occ_orbitals, "virt_orbitals": virt_orbitals, "potentials": potentials, "occ_energy": occ_energy, "virt_energy": virt_energy, "times": times, "weights": weights}


def reference(occ_orbitals, virt_orbitals, potentials, occ_energy, virt_energy, times, weights):
    pot_wide = potentials.astype(jnp.float32)
    contract = (((1,), (1,)), ((), ()))

    def one_time(moment):
        occ_half = (occ_orbitals.astype(jnp.float32) * jnp.exp(0.5 * moment * occ_energy)).astype(jnp.bfloat16)
        virt_half = (virt_orbitals.astype(jnp.float32) * jnp.exp(-0.5 * moment * virt_energy)).astype(jnp.bfloat16)
        green_occ = lax.dot_general(occ_half, occ_half, contract, preferred_element_type=jnp.float32)
        green_virt = lax.dot_general(virt_half, virt_half, contract, preferred_element_type=jnp.float32)
        response = (-(green_occ * green_virt)).astype(jnp.bfloat16)
        applied = jnp.dot(response, potentials, preferred_element_type=jnp.float32)
        return lax.dot_general(pot_wide, applied, (((0,), (0,)), ((), ())), precision=lax.Precision.HIGHEST)

    projected = lax.map(one_time, times)
    return jnp.einsum("wt,tab->wab", weights.astype(jnp.float32), projected, precision=lax.Precision.HIGHEST)
```

```python
import functools

import jax
import jax.numpy as jnp
from jax import lax
from jax.experimental import pallas as pl
from jax.experimental.pallas import tpu as pltpu
from jax.sharding import PartitionSpec as P


NT = (((1,), (1,)), ((), ()))
TN = (((0,), (0,)), ((), ()))


def exchange(value, axis, flip):
    count = lax.axis_size(axis)
    return lax.ppermute(value, axis, [(i, i ^ flip) for i in range(count)])


def shift(value, axis, steps):
    count = lax.axis_size(axis)
    return lax.ppermute(value, axis, [(i, (i + steps) % count) for i in range(count)])


def pair_kernel(blocks, groups, n_times, occ_steps, pack, carry, scal_ref, *refs):
    n = len(blocks)
    rows = refs[:n]
    pots = refs[n : 2 * n]
    f_ref = refs[2 * n]
    at = 2 * n + 1
    carry_ref = refs[at] if carry else None
    at += 1 if carry else 0
    out_ref = refs[at]
    accs = refs[at + 1 :]
    k = pl.program_id(0)
    kind = (k >= occ_steps).astype(jnp.int32)

    @pl.when(k == 0)
    def _():
        for acc in accs:
            acc[...] = jnp.zeros_like(acc)

    for t in range(n_times):
        factor = f_ref[t : t + 1, :]
        scaled = [(r[...].astype(jnp.float32) * factor).astype(jnp.bfloat16) for r in rows]
        for acc, (left, right, _) in zip(accs, groups):
            lhs = jnp.concatenate([scaled[i] for i in left], axis=0)
            rhs = jnp.concatenate([scaled[i] for i in right], axis=0)
            acc[kind, t] += lax.dot_general(lhs, rhs, NT, preferred_element_type=jnp.float32)

    @pl.when(k == pl.num_programs(0) - 1)
    def _():
        for t in range(n_times):
            total = None
            for acc, (left, right, half) in zip(accs, groups):
                response = (-(acc[0, t] * acc[1, t])).astype(jnp.bfloat16)
                near = jnp.concatenate([pots[i][...] for i in left], axis=0)
                far = jnp.concatenate([pots[i][...] for i in right], axis=0)
                if half:
                    far = far * jnp.bfloat16(0.5)
                applied = jnp.dot(response, far, preferred_element_type=jnp.float32)
                high = applied.astype(jnp.bfloat16)
                low = (applied - high.astype(jnp.float32)).astype(jnp.bfloat16)
                part = lax.dot_general(near, high, TN, preferred_element_type=jnp.float32)
                part = part + lax.dot_general(near, low, TN, preferred_element_type=jnp.float32)
                total = part if total is None else total + part
            if carry:
                total = total + carry_ref[t]
            if pack:
                h = total.shape[0] // 2
                out_ref[t, 0:h] = total[:h, :h] + total[:h, :h].T
                out_ref[t, h : 2 * h] = total[:h, h:] + total[h:, :h].T
                out_ref[t, 2 * h : 3 * h] = total[h:, h:] + total[h:, h:].T
            else:
                out_ref[t] = total


def pair_call(scalars, operands, groups, factors, n_occ, n_pot, carry=None, pack=False):
    n_times, width = factors.shape
    step = 1024
    while n_occ % step or width % step:
        step //= 2
    pot_at = width // n_pot
    row_specs, pot_specs, arrays = [], [], []
    for array, height, slot in operands:
        def at(k, s, slot=slot):
            return (0 if slot is None else s[slot], k)

        def pot_index(k, s, slot=slot):
            return (0 if slot is None else s[slot], pot_at)

        row_specs.append(pl.BlockSpec((height, step), at))
        pot_specs.append(pl.BlockSpec((height, n_pot), pot_index))
        arrays.append(array)
    heights = [o[1] for o in operands]
    acc_shapes = [
        (2, n_times, sum(heights[i] for i in left), sum(heights[i] for i in right))
        for left, right, _ in groups
    ]
    in_specs = row_specs + pot_specs + [pl.BlockSpec((n_times, step), lambda k, s: (0, k))]
    inputs = arrays + arrays + [factors]
    if carry is not None:
        in_specs.append(pl.BlockSpec(carry.shape, lambda k, s: (0, 0, 0)))
        inputs.append(carry)
    if pack:
        out = (n_times, 3 * n_pot // 2, n_pot // 2)
    else:
        out = (n_times, n_pot, n_pot)
    flops = sum(2 * a[1] * a[2] * a[3] * width for a in acc_shapes)
    return pl.pallas_call(
        functools.partial(
            pair_kernel, operands, groups, n_times, n_occ // step, pack, carry is not None
        ),
        grid_spec=pltpu.PrefetchScalarGridSpec(
            num_scalar_prefetch=1,
            grid=(width // step,),
            in_specs=in_specs,
            out_specs=pl.BlockSpec(out, lambda k, s: (0, 0, 0)),
            scratch_shapes=[pltpu.VMEM(a, jnp.float32) for a in acc_shapes],
        ),
        out_shape=jax.ShapeDtypeStruct(out, jnp.float32),
        compiler_params=pltpu.CompilerParams(dimension_semantics=("arbitrary",)),
        cost_estimate=pl.CostEstimate(
            flops=flops, transcendentals=0, bytes_accessed=2 * width * sum(heights)
        ),
    )(scalars, *inputs)


def columns_body(occ_orbitals, virt_orbitals, potentials, occ_energy, virt_energy, times, weights):
    planes = lax.axis_size("tau")
    rows, n_occ = occ_orbitals.shape
    n_pot = potentials.shape[1]
    part = rows // planes
    place = lax.axis_index("pts")
    core = place & 1
    at_x = (place >> 1) & 1
    at_y = (place >> 2) & 1
    plane = lax.axis_index("tau")

    def rows_of(index):
        return jnp.concatenate(
            [
                lax.dynamic_slice_in_dim(a, index * part, part, 0)
                for a in (occ_orbitals, virt_orbitals, potentials)
            ],
            axis=1,
        )

    x_part = plane ^ (2 * at_y)
    y_send = rows_of(plane)
    x_send = rows_of(x_part)

    mine = jnp.concatenate([times, weights[:, 0]])
    heard = [mine] + [shift(mine, "tau", s) for s in range(1, planes)]
    table = jnp.take(jnp.stack(heard), (plane - jnp.arange(planes)) % planes, axis=0)
    half = planes // 2
    near_table = lax.dynamic_slice_in_dim(table, core * half, half, 0)
    far_table = lax.dynamic_slice_in_dim(table, (1 - core) * half, half, 0)
    moments = near_table[:, :1]

    chunks = 3
    size = part // chunks
    x_mine = exchange(x_send, "pts", 2)
    y_chunks, e_chunks = [], []
    for i in range(chunks):
        y_chunks.append(exchange(y_send[i * size : (i + 1) * size], "pts", 4))
    for i in range(chunks):
        e_chunks.append(exchange(y_chunks[i], "tau", 1))
    own = jnp.concatenate([occ_orbitals, virt_orbitals, potentials], axis=1)
    own_far = exchange(own, "pts", 1)
    y_mine = jnp.concatenate(y_chunks, axis=0)
    x_far = exchange(x_mine, "pts", 1)
    y_far = exchange(y_mine, "pts", 1)
    e_mine = jnp.concatenate(e_chunks, axis=0)
    e_far = exchange(e_mine, "pts", 1)

    factors = jnp.concatenate(
        [
            jnp.exp(0.5 * moments * occ_energy[None]),
            jnp.exp(-0.5 * moments * virt_energy[None]),
        ],
        axis=1,
    )
    scalars = jnp.stack([plane, (x_part >> 1) ^ at_x, (plane >> 1) ^ at_y]).astype(jnp.int32)
    call = functools.partial(pair_call, scalars, factors=factors, n_occ=n_occ, n_pot=n_pot)

    total = call(
        [(own, part, 0), (own_far, part, 0), (own, rows, None), (own_far, rows, None)],
        [((0, 1), (2, 3), True)],
    )
    wide = rows // 2
    total = call(
        [
            (x_mine, part, None),
            (x_far, part, None),
            (y_mine, part, None),
            (y_far, part, None),
            (own, wide, 1),
            (own_far, wide, 1),
            (own, wide, 2),
            (own_far, wide, 2),
        ],
        [((0, 1), (4, 5, 2, 3), False), ((2, 3), (6, 7), False)],
        carry=total,
    )
    packed = call(
        [(x_mine, part, None), (x_far, part, None), (e_mine, part, None), (e_far, part, None)],
        [((0, 1), (2, 3), False)],
        carry=total,
        pack=True,
    )

    columns = lax.axis_size("pts") // 2
    column = place >> 1
    piece = packed.shape[1] // columns

    def piece_of(value, index):
        return lax.dynamic_slice_in_dim(value, index * piece, piece, 1)

    summed = piece_of(packed, column)
    for flip in range(1, columns):
        summed = summed + exchange(piece_of(packed, column ^ flip), "pts", 2 * flip)
    short = piece // 2
    keep = lax.dynamic_slice_in_dim(summed, core * short, short, 1)
    other = exchange(lax.dynamic_slice_in_dim(summed, (1 - core) * short, short, 1), "pts", 1)
    contribution = jnp.zeros((planes,) + keep.shape[1:], jnp.float32)
    for t in range(half):
        contribution = contribution + near_table[t, 1:][:, None, None] * keep[t][None]
        contribution = contribution + far_table[t, 1:][:, None, None] * other[t][None]
    result = lax.dynamic_index_in_dim(contribution, plane, 0, keepdims=False)
    for s in range(1, planes):
        block = lax.dynamic_index_in_dim(contribution, (plane + s) % planes, 0, keepdims=False)
        result = result + shift(block, "tau", s)
    result_far = exchange(result, "pts", 1)
    first = jnp.where(core == 0, result, result_far)
    second = jnp.where(core == 0, result_far, result)
    here = jnp.concatenate([first, second], axis=0)
    pieces = [here] + [exchange(here, "pts", 2 * flip) for flip in range(1, columns)]
    full = jnp.zeros((columns,) + here.shape, jnp.float32)
    for flip in range(columns):
        full = lax.dynamic_update_index_in_dim(full, pieces[flip], column ^ flip, 0)
    full = full.reshape(packed.shape[1:])
    h = n_pot // 2
    upper, cross, lower = full[:h], full[h : 2 * h], full[2 * h :]
    return jnp.block([[upper, cross], [cross.T, lower]])[None]


def ring_body(occ_orbitals, virt_orbitals, potentials, occ_energy, virt_energy, times, weights):
    half_cycle = lax.axis_size("pts") // 2
    n_occ = occ_orbitals.shape[1]
    n_virt = virt_orbitals.shape[1]
    moment = times[0]
    occ_factor = jnp.exp(0.5 * moment * occ_energy)
    virt_factor = jnp.exp(-0.5 * moment * virt_energy)
    occ_scaled = (occ_orbitals.astype(jnp.float32) * occ_factor).astype(jnp.bfloat16)
    virt_scaled = (virt_orbitals.astype(jnp.float32) * virt_factor).astype(jnp.bfloat16)
    pot_wide = potentials.astype(jnp.float32)

    def pair_block(far_occ, far_virt, far_pot):
        green_occ = lax.dot_general(occ_scaled, far_occ, NT, preferred_element_type=jnp.float32)
        green_virt = lax.dot_general(virt_scaled, far_virt, NT, preferred_element_type=jnp.float32)
        response = (-(green_occ * green_virt)).astype(jnp.bfloat16)
        applied = jnp.dot(response, far_pot, preferred_element_type=jnp.float32)
        return lax.dot_general(pot_wide, applied, TN, precision=lax.Precision.HIGHEST)

    arrived = jnp.concatenate([occ_scaled, virt_scaled, potentials], axis=1)
    summed_pairs = pair_block(occ_scaled, virt_scaled, potentials)
    for offset in range(1, half_cycle + 1):
        arrived = shift(arrived, "pts", -1)
        pair_sum = pair_block(
            arrived[:, :n_occ], arrived[:, n_occ : n_occ + n_virt], arrived[:, n_occ + n_virt :]
        )
        summed_pairs = summed_pairs + pair_sum
        if offset < half_cycle:
            summed_pairs = summed_pairs + pair_sum.T
    all_pairs = lax.psum(summed_pairs, "pts")
    weighted = weights[:, 0][:, None, None] * all_pairs[None]
    return lax.psum_scatter(weighted, "tau", scatter_dimension=0, tiled=True)


def solution(mesh):
    columns = mesh.shape["pts"] // 2
    body = columns_body if columns == 4 and mesh.shape["tau"] == columns else ring_body
    return jax.shard_map(
        body,
        mesh=mesh,
        in_specs=(
            P("pts", None),
            P("pts", None),
            P("pts", None),
            P(),
            P(),
            P("tau"),
            P(None, "tau"),
        ),
        out_specs=P("tau", None, None),
        check_vma=False,
    )
```
